32 devices in a mesh: row: 8 (over y, x, core), col: 4 (over z).
Axes of the slice: x: 2, y: 2, z: 4, core: 2. Of those that a mesh axis runs over, the one named last changes fastest.
Arguments:
- residual: float32 [8, 2048, 128], P(None, 'row'), may hold values from -6 to 6
- diag_inverse: bfloat16 [2, 2048, 2048], P(None, 'col', 'row'), as said below
- panels: bfloat16 [2, 8, 2048, 2048], P(None, None, 'row', 'col'), may hold values from -0.125 to 0.125
- first_block: int32 [1], replicated, may hold values from 0 to 6
- probe_solved: bfloat16 [8, 2048, 128], P(None, 'row'), may hold values from -6 to 6
- genotypes: bfloat16 [8, 2048, 16384], P(None, 'row', 'col'), may hold values from -6 to 6
- annotation: int32 [16384], P('col'), may hold values from 0 to 7
Outputs:
- trailing: float32 [8, 2048, 128], P(None, 'row')
- solved: float32 [2, 2048, 128], P(None, 'col')
- grm_products: bfloat16 [8, 2048, 8, 128], P(None, 'row', 'col')
The draws below stay inside these ranges and needn't reach their ends.
Inputs may be any that keep to these rules, and one draw needn't show every extreme that they name: The two solve steps are blocks first_block and first_block + 1. diag_inverse is lower triangular in each of its two blocks.
All inputs are finite; a program needn't handle non-finite values.
Results may differ from the reference program's by a relative error of at most 0.0085.
Values may be sent and summed in bfloat16 or wider, within the bound.
No kernel may reach another device: no remote copies, remote signals or barrier semaphores. Data moves between devices by JAX's collectives and lax.ppermute only.
A program may use at most 128 MiB of HBM per device.

```python
import jax
import jax.numpy as jnp
from jax import lax

B = 2048
R = 128
A = 8
SNPS = 16384
NBLK = 8


def draw_diag_inverse(key, part):
    key_off, key_diag = jax.random.split(key)
    rows_idx = lax.broadcasted_iota(jnp.int32, (2, B, B), 1)
    cols_idx = lax.broadcasted_iota(jnp.int32, (2, B, B), 2)
    off_part = jax.random.normal(key_off, (2, B, B), jnp.float32) / jnp.sqrt(jnp.float32(B))
    diag_part = jax.random.uniform(key_diag, (2, B, B), jnp.float32, 0.7, 1.3)
    lower = jnp.where(rows_idx > cols_idx, off_part, jnp.where(rows_idx == cols_idx, diag_part, 0.0))
    return lower.astype(jnp.bfloat16)


def place_ends(drawn, own_key, smallest, top_value):
    dims = drawn.shape
    spot = [jax.random.randint(jax.random.fold_in(own_key, axis), (), 0, dims[axis]) for axis in range(len(dims))]
    drawn = drawn.at[tuple(spot)].set(smallest)
    longest = dims.index(max(dims))
    spot[longest] = (spot[longest] + 1) % dims[longest]
    return drawn.at[tuple(spot)].set(top_value)


def level_of(key, dims, cuts, low, high):
    factor_of, own = 1.0, jax.random.fold_in(key, 6)
    for dim, shards_of in cuts:
        draws = jnp.exp(jax.random.uniform(jax.random.fold_in(own, dim), (shards_of,), jnp.float32, low / len(cuts), high / len(cuts)))
        factor_of = factor_of * jnp.repeat(draws, dims[dim] // shards_of).reshape([-1 if axis == dim else 1 for axis in range(len(dims))])
    return factor_of


def scatter_about(stream_key, dims, spread, most, shards=(), held_as=jnp.bfloat16):
    drawn = spread * jax.random.normal(stream_key, dims, jnp.float32)
    if shards:
        drawn = drawn * level_of(stream_key, dims, shards, -0.22, 0.18)
    return jnp.clip(drawn, -most, most).astype(held_as)


def setup_inputs(seed: int = 0) -> dict:
    arg_keys = jax.random.split(jax.random.key(seed), 8)
    return {
        "residual": scatter_about(arg_keys[0], (NBLK, B, R), 1.0, 6.0, ((1, 8),), jnp.float32),
        "diag_inverse": draw_diag_inverse(jax.random.fold_in(arg_keys[7], 71), 0),
        "panels": scatter_about(arg_keys[2], (2, NBLK, B, B), B ** -0.5, 0.125, ((2, 8), (3, 4))),
        "first_block": jax.random.randint(arg_keys[3], (1,), 0, NBLK - 1).astype(jnp.int32),
        "probe_solved": scatter_about(arg_keys[4], (NBLK, B, R), 1.0, 6.0, ((1, 8),)),
        "genotypes": scatter_about(arg_keys[5], (NBLK, B, SNPS), 1.0, 6.0, ((1, 8), (2, 4))),
        "annotation": place_ends(jax.random.randint(arg_keys[6], (SNPS,), 0, A), jax.random.fold_in(arg_keys[6], 1), 0, A - 1).astype(jnp.int32),
    }


def reference(residual, diag_inverse, panels, first_block, probe_solved, genotypes, annotation):
    block_now = first_block[0].astype(jnp.int32)
    positions = jnp.arange(NBLK, dtype=jnp.int32)
    current = residual
    solved_list = []
    for section in range(2):
        target = block_now + section
        row_values = lax.dynamic_index_in_dim(current, target, 0, keepdims=False)
        solved_now = jnp.dot(diag_inverse[section], row_values.astype(jnp.bfloat16), preferred_element_type=jnp.float32)
        update = jnp.dot(panels[section].reshape(NBLK * B, B), solved_now.astype(jnp.bfloat16), preferred_element_type=jnp.float32).reshape(NBLK, B, R)
        keep_mask = (positions > target).astype(jnp.float32)[:, None, None]
        current = current - keep_mask * update
        solved_list.append(solved_now)
    flat_geno = genotypes.reshape(NBLK * B, SNPS)
    loadings = jnp.dot(flat_geno.T, probe_solved.reshape(NBLK * B, R), preferred_element_type=jnp.float32)
    rounded = (loadings * (1.0 / SNPS)).astype(jnp.bfloat16)
    onehot = annotation[:, None] == jnp.arange(A, dtype=jnp.int32)[None, :]
    weights = jnp.where(onehot[:, :, None], rounded[:, None, :], jnp.zeros((), jnp.bfloat16)).reshape(SNPS, A * R)
    grm_products = jnp.dot(flat_geno, weights, preferred_element_type=jnp.float32).reshape(NBLK, B, A, R).astype(jnp.bfloat16)
    return current, jnp.stack(solved_list), grm_products
```

```python
import jax
import jax.numpy as jnp
from jax import lax
from jax.experimental import pallas as pl
from jax.experimental.pallas import tpu as pltpu
from jax.sharding import PartitionSpec as P

A = 8
BF = jnp.bfloat16
F32 = jnp.float32


def project_kernel(core_ref, probe_ref, geno_ref, *rest):
    outs, turned = rest[:-1], rest[-1]

    @pl.when(pl.program_id(0) == 0)
    def _():
        turned[...] = probe_ref[...].T

    acc = jnp.dot(turned[...], geno_ref[...], preferred_element_type=F32)
    core = core_ref[0]
    half = acc.shape[0] // 2
    quarter = half // 2
    for h in range(2):
        low = acc[h * half : h * half + quarter]
        high = acc[h * half + quarter : (h + 1) * half]
        outs[2 * h][...] = jnp.where(core == 0, low, high)
        outs[2 * h + 1][...] = jnp.where(core == 0, high, low).astype(BF)


def project(core, probe, geno):
    rows, snps = geno.shape
    rhs = probe.shape[1]
    tile = min(512, snps)
    quarter = rhs // 4
    out_spec = pl.BlockSpec((quarter, tile), lambda i, c: (0, i))
    shapes = []
    for _ in range(2):
        shapes += [jax.ShapeDtypeStruct((quarter, snps), F32), jax.ShapeDtypeStruct((quarter, snps), BF)]
    return pl.pallas_call(
        project_kernel,
        grid_spec=pltpu.PrefetchScalarGridSpec(
            num_scalar_prefetch=1,
            grid=(snps // tile,),
            in_specs=[
                pl.BlockSpec((rows, rhs), lambda i, c: (0, 0)),
                pl.BlockSpec((rows, tile), lambda i, c: (0, i)),
            ],
            out_specs=[out_spec] * 4,
            scratch_shapes=[pltpu.VMEM((rhs, rows), BF)],
        ),
        out_shape=shapes,
        name="project",
    )(core, probe, geno)


def annotate_kernel(slices, per_slice, ids_ref, load_ref, ann_ref, geno_ref, *rest):
    outs, weights = rest[:-1], rest[-1]
    width = load_ref.shape[0]

    @pl.when(pl.program_id(0) == 0)
    def _():
        for s in range(slices):
            for a in range(per_slice):
                mask = (ann_ref[...] == ids_ref[s] * per_slice + a).astype(F32).astype(BF)
                spot = (s * per_slice + a) * width
                weights[spot : spot + width, :] = load_ref[...] * mask

    acc = lax.dot_general(
        geno_ref[...], weights[...], (((1,), (1,)), ((), ())), preferred_element_type=F32
    )
    wide = per_slice * width
    for s in range(slices):
        outs[s][...] = acc[:, s * wide : (s + 1) * wide].astype(BF)


def annotate(ids, load, ann, geno, per_slice):
    rows, snps = geno.shape
    slices = ids.shape[0]
    width = load.shape[0]
    tile = min(256, rows)
    wide = per_slice * width

    def kernel(*refs):
        annotate_kernel(slices, per_slice, *refs)

    return pl.pallas_call(
        kernel,
        grid_spec=pltpu.PrefetchScalarGridSpec(
            num_scalar_prefetch=1,
            grid=(rows // tile,),
            in_specs=[
                pl.BlockSpec((width, snps), lambda i, c: (0, 0)),
                pl.BlockSpec((1, snps), lambda i, c: (0, 0)),
                pl.BlockSpec((tile, snps), lambda i, c: (i, 0)),
            ],
            out_specs=[pl.BlockSpec((tile, wide), lambda i, c: (i, 0))] * slices,
            scratch_shapes=[pltpu.VMEM((slices * wide, snps), BF)],
        ),
        out_shape=[jax.ShapeDtypeStruct((rows, wide), BF)] * slices,
        name="annotate",
    )(ids, load, ann, geno)


def flip(x, axis, size, bits):
    return lax.ppermute(x, axis, [(i, i ^ bits) for i in range(size)])


def pick(index, table, choose):
    distinct = sorted(set(table))
    out = choose(distinct[0])
    for p in distinct[1:]:
        here = False
        for i, q in enumerate(table):
            if q == p:
                here = here | (index == i)
        out = jnp.where(here, choose(p), out)
    return out


def make_shards(nr, nc):
    chips = nr // 2

    def row_sum(x, core):
        half = x.shape[0] // 2
        low, high = x[:half], x[half:]
        mine = jnp.where(core == 0, low, high)
        other = jnp.where(core == 0, high, low).astype(BF)
        mine = mine + flip(other, "row", nr, 1).astype(F32)
        sent = mine.astype(BF)
        for q in range(1, chips):
            mine = mine + flip(sent, "row", nr, 2 * q).astype(F32)
        other = flip(mine, "row", nr, 1)
        return jnp.concatenate(
            [jnp.where(core == 0, mine, other), jnp.where(core == 0, other, mine)], axis=0
        )

    def col_sum_small(x):
        sent = x.astype(BF)
        for q in range(1, nc):
            x = x + flip(sent, "col", nc, q).astype(F32)
        return x

    def col_sum_large(x, col):
        bits = []
        b = 1
        while b < nc:
            bits.append(b)
            b *= 2
        for b in bits:
            half = x.shape[0] // 2
            up = (col & b) != 0
            mine = jnp.where(up, x[half:], x[:half])
            other = jnp.where(up, x[:half], x[half:])
            x = (mine.astype(F32) + flip(other, "col", nc, b).astype(F32)).astype(BF)
        for b in reversed(bits):
            up = (col & b) != 0
            other = flip(x, "col", nc, b)
            x = jnp.concatenate([jnp.where(up, other, x), jnp.where(up, x, other)], axis=0)
        return x

    def loadings_half(keep, sent, core, row, scale):
        chip = row // 2
        mine = keep + flip(sent, "row", nr, 1).astype(F32)
        part = mine.shape[0] // chips
        parts = mine.reshape(chips, part, mine.shape[1])
        total = lax.dynamic_index_in_dim(parts, chip, 0, keepdims=False)
        for q in range(1, chips):
            piece = lax.dynamic_index_in_dim(parts, chip ^ q, 0, keepdims=False).astype(BF)
            total = total + flip(piece, "row", nr, 2 * q).astype(F32)
        total = (total * scale).astype(BF)
        got = [total] + [flip(total, "row", nr, 2 * q) for q in range(1, chips)]
        tables = [[c ^ q for c in range(chips)] for q in range(chips)]
        mine = jnp.concatenate([pick(chip, t, lambda p: got[p]) for t in tables], axis=0)
        other = flip(mine, "row", nr, 1)
        return jnp.concatenate(
            [jnp.where(core == 0, mine, other), jnp.where(core == 0, other, mine)], axis=0
        )

    def line_scatter(own, col):
        near = nc // 2

        def position(z, s):
            return nc - 1 - s if z < near else s

        def right_table(t):
            return [position(z, nc - 1 - t + z) if z <= t else None for z in range(nc)]

        def left_table(t):
            return [position(z, t - (nc - 1 - z)) if nc - 1 - z <= t else None for z in range(nc)]

        def filled(table):
            some = [p for p in table if p is not None][0]
            return [some if p is None else p for p in table]

        from_left = from_right = None
        for t in range(nc - 1):
            right = [(z, z + 1) for z in range(nc) if z <= t]
            left = [(z, z - 1) for z in range(nc) if nc - 1 - z <= t]
            send_right = pick(col, filled(right_table(t)), lambda p: own[p])
            send_left = pick(col, filled(left_table(t)), lambda p: own[p])
            if t > 0:
                send_right = (send_right.astype(F32) + from_left.astype(F32)).astype(BF)
                send_left = (send_left.astype(F32) + from_right.astype(F32)).astype(BF)
            from_left = lax.ppermute(send_right, "col", right)
            from_right = lax.ppermute(send_left, "col", left)
        last = pick(col, [position(z, z) for z in range(nc)], lambda p: own[p])
        return last.astype(F32) + from_left.astype(F32) + from_right.astype(F32)

    def shards(residual, diag_inverse, panels, first_block, probe_solved, genotypes, annotation):
        nblk, g, rhs = residual.shape
        row = lax.axis_index("row")
        col = lax.axis_index("col")
        core = row % 2
        scale = 1.0 / (annotation.shape[0] * nc)
        geno = genotypes.reshape(-1, genotypes.shape[2])
        probe = probe_solved.reshape(-1, rhs)
        block_now = first_block[0]

        pieces = project(core[None].astype(jnp.int32), probe, geno)

        first_rows = lax.dynamic_index_in_dim(residual, block_now, 0, keepdims=False)
        first = row_sum(jnp.dot(diag_inverse[0], first_rows.astype(BF), preferred_element_type=F32), core)
        first_bf = first.astype(BF)

        ann = annotation.reshape(1, -1)
        per_slice = A // nc
        near = col < nc // 2
        order = [jnp.where(near, nc - 1 - p, p) for p in range(nc)]
        summed = []
        for h in range(2):
            load = loadings_half(pieces[2 * h], pieces[2 * h + 1], core, row, scale)
            own = []
            for p in range(0, nc, 2):
                ids = jnp.stack(order[p : p + 2]).astype(jnp.int32)
                own += annotate(ids, load, ann, geno, per_slice)
            summed.append(line_scatter(own, col))

        next_panel = lax.dynamic_index_in_dim(panels[0], block_now + 1, 0, keepdims=False)
        next_sum = col_sum_small(jnp.dot(next_panel, first_bf, preferred_element_type=F32))
        second_rows = lax.dynamic_index_in_dim(residual, block_now + 1, 0, keepdims=False) - next_sum
        second = row_sum(
            jnp.dot(diag_inverse[1], second_rows.astype(BF), preferred_element_type=F32), core
        )
        second_bf = second.astype(BF)
        late = jnp.arange(2, nblk, dtype=jnp.int32)
        keep_first = (late > block_now).astype(F32)[:, None, None]
        keep_second = (late > block_now + 1).astype(F32)[:, None, None]
        both = keep_first * jnp.einsum(
            "ngc,cr->ngr", panels[0, 2:], first_bf, preferred_element_type=F32
        ) + keep_second * jnp.einsum(
            "ngc,cr->ngr", panels[1, 2:], second_bf, preferred_element_type=F32
        )
        update = col_sum_large(both.astype(BF).reshape(-1, rhs), col).reshape(nblk - 2, g, rhs)
        current = jnp.concatenate([residual[:2], residual[2:] - update.astype(F32)], axis=0)
        spot = jnp.arange(nblk, dtype=jnp.int32)[:, None, None] == block_now + 1
        current = jnp.where(spot, second_rows[None], current)

        half = rhs // 2
        products = jnp.stack(summed, axis=1)
        products = products.reshape(nblk, g, 2, per_slice, half)
        products = jnp.swapaxes(products, 2, 3).reshape(nblk, g, per_slice, rhs).astype(BF)
        return current, jnp.stack([first, second]), products

    return shards


def solution(mesh):
    in_specs = (
        P(None, "row", None),
        P(None, "col", "row"),
        P(None, None, "row", "col"),
        P(),
        P(None, "row", None),
        P(None, "row", "col"),
        P("col"),
    )
    out_specs = (P(None, "row", None), P(None, "col", None), P(None, "row", "col", None))
    shards = make_shards(mesh.shape["row"], mesh.shape["col"])
    return jax.shard_map(shards, mesh=mesh, in_specs=in_specs, out_specs=out_specs, check_vma=False)
```

```python
import jax
import jax.numpy as jnp
from jax import lax
from jax.experimental import pallas as pl
from jax.experimental.pallas import tpu as pltpu
from jax.sharding import PartitionSpec as P


A = 8
BF = jnp.bfloat16
F32 = jnp.float32


def project_kernel(chunks, block_ref, row_ref, probe_hbm, inverse_hbm, residual_hbm, geno_hbm, *rest):
    outs, (geno, probe, inverse, residual, turned, sems) = rest[:4], rest[4:]
    snps = geno.shape[1]
    tile = snps // chunks
    depth = min(3, chunks)

    def copy(i):
        spot = pl.ds(i * tile, tile)
        return pltpu.make_async_copy(geno_hbm.at[:, spot], geno.at[:, spot], sems.at[i])

    inverse_copy = pltpu.make_async_copy(inverse_hbm.at[0], inverse, sems.at[chunks])
    residual_copy = pltpu.make_async_copy(
        residual_hbm.at[block_ref[0]], residual, sems.at[chunks + 1]
    )
    probe_copy = pltpu.make_async_copy(probe_hbm, probe, sems.at[chunks + 2])
    inverse_copy.start()
    residual_copy.start()
    probe_copy.start()
    for i in range(depth):
        copy(i).start()
    core = row_ref[0] % 2
    chips, part = outs[0].shape[0], outs[0].shape[1]
    span = chips * part

    def spread(h, low, high, lanes):
        mine = jnp.where(core == 0, low, high)
        other = jnp.where(core == 0, high, low).astype(BF)
        for q in range(chips):
            rows = slice(q * part, (q + 1) * part)
            outs[2 * h][q, :, lanes] = mine[rows]
            outs[2 * h + 1][q, :, lanes] = other[rows]

    inverse_copy.wait()
    residual_copy.wait()
    solved = jnp.dot(inverse[...], residual[...].astype(BF), preferred_element_type=F32)
    rhs = solved.shape[1]
    for j in range(solved.shape[0] // (2 * span)):
        lanes = slice(snps + j * rhs, snps + (j + 1) * rhs)
        top = 2 * span * j
        spread(0, solved[top : top + span], solved[top + span : top + 2 * span], lanes)
    probe_copy.wait()
    turned[...] = probe[...].T
    for i in range(chunks):
        copy(i).wait()
        if i + depth < chunks:
            copy(i + depth).start()
        lanes = slice(i * tile, (i + 1) * tile)
        acc = jnp.dot(turned[...], geno[:, lanes], preferred_element_type=F32)
        for h in range(2):
            top = 2 * span * h
            spread(h, acc[top : top + span], acc[top + span : top + 2 * span], lanes)


def project(block, row, probe, inverse, residual, geno, chips):
    rows, snps = geno.shape
    rhs = probe.shape[1]
    part = rhs // (4 * chips)
    chunks = 8
    _, m, g = inverse.shape
    extra = m * rhs // (rhs // 2)
    shapes = []
    for wide in (snps + extra, snps):
        shapes += [
            jax.ShapeDtypeStruct((chips, part, wide), F32),
            jax.ShapeDtypeStruct((chips, part, wide), BF),
        ]

    def kernel(*refs):
        project_kernel(chunks, *refs)

    return pl.pallas_call(
        kernel,
        grid_spec=pltpu.PrefetchScalarGridSpec(
            num_scalar_prefetch=2,
            grid=(1,),
            in_specs=[pl.BlockSpec(memory_space=pltpu.HBM)] * 4,
            out_specs=[pl.BlockSpec(s.shape, lambda i, b, c: (0, 0, 0)) for s in shapes],
            scratch_shapes=[
                pltpu.VMEM((rows, snps), BF),
                pltpu.VMEM((rows, rhs), BF),
                pltpu.VMEM((m, g), BF),
                pltpu.VMEM((g, rhs), F32),
                pltpu.VMEM((rhs, rows), BF),
                pltpu.SemaphoreType.DMA((chunks + 3,)),
            ],
        ),
        out_shape=shapes,
        cost_estimate=pl.CostEstimate(
            flops=2 * rows * snps * rhs, bytes_accessed=2 * rows * snps, transcendentals=0
        ),
        name="project",
    )(block, row, probe, inverse, residual, geno)


def annotate_kernel(ids_of, slices, per_slice, row_ref, col_ref, mine_ref, other_ref, ann_ref, geno_ref, *rest):
    outs, (load, weights) = rest[:slices], rest[slices:]
    chips, part, _ = mine_ref.shape
    width = load.shape[0]

    @pl.when(pl.program_id(0) == 0)
    def _():
        core, chip = row_ref[0] % 2, row_ref[0] // 2
        ids = ids_of(col_ref[0])
        for q in range(chips):
            mine = mine_ref[q ^ chip].astype(F32)
            other = other_ref[q ^ chip].astype(F32)
            load[q * part : (q + 1) * part, :] = jnp.where(core == 0, mine, other)
            low = width // 2 + q * part
            load[low : low + part, :] = jnp.where(core == 0, other, mine)
        for s in range(slices):
            for a in range(per_slice):
                here = ann_ref[...] == ids[s] * per_slice + a
                spot = (s * per_slice + a) * width
                weights[spot : spot + width, :] = jnp.where(here, load[...], 0.0).astype(BF)

    wide = per_slice * width
    acc = lax.dot_general(
        geno_ref[...], weights[...], (((1,), (1,)), ((), ())), preferred_element_type=F32
    )
    for s in range(slices):
        outs[s][...] = acc[:, s * wide : (s + 1) * wide].astype(BF)


def annotate(ids_of, slices, row, col, mine, other, ann, geno, per_slice):
    rows, snps = geno.shape
    chips, part, _ = mine.shape
    width = 2 * chips * part
    wide = per_slice * width
    tile = rows // 2

    def kernel(*refs):
        annotate_kernel(ids_of, slices, per_slice, *refs)

    return pl.pallas_call(
        kernel,
        grid_spec=pltpu.PrefetchScalarGridSpec(
            num_scalar_prefetch=2,
            grid=(rows // tile,),
            in_specs=[
                pl.BlockSpec((chips, part, snps), lambda i, c, d: (0, 0, 0)),
                pl.BlockSpec((chips, part, snps), lambda i, c, d: (0, 0, 0)),
                pl.BlockSpec((1, snps), lambda i, c, d: (0, 0)),
                pl.BlockSpec((tile, snps), lambda i, c, d: (i, 0)),
            ],
            out_specs=[pl.BlockSpec((tile, wide), lambda i, c, d: (i, 0))] * slices,
            scratch_shapes=[pltpu.VMEM((width, snps), F32), pltpu.VMEM((slices * wide, snps), BF)],
        ),
        out_shape=[jax.ShapeDtypeStruct((rows, wide), BF)] * slices,
        cost_estimate=pl.CostEstimate(
            flops=2 * rows * snps * slices * wide, bytes_accessed=2 * rows * snps, transcendentals=0
        ),
        name="annotate",
    )(row, col, mine, other, ann, geno)


def unfold(row, mine, other, snps, rhs):
    chips, part, lanes = mine.shape
    width = 2 * chips * part
    pieces = (lanes - snps) // rhs

    def kernel(row_ref, *refs):
        mine_refs, other_refs, out = refs[:pieces], refs[pieces : 2 * pieces], refs[-1]
        core, chip = row_ref[0] % 2, row_ref[0] // 2
        for j in range(pieces):
            for q in range(chips):
                mine_now = mine_refs[j][q ^ chip].astype(F32)
                other_now = other_refs[j][q ^ chip].astype(F32)
                spot = j * width + q * part
                out[spot : spot + part, :] = jnp.where(core == 0, mine_now, other_now)
                spot += width // 2
                out[spot : spot + part, :] = jnp.where(core == 0, other_now, mine_now)

    first = snps // rhs
    specs = [
        pl.BlockSpec((chips, part, rhs), lambda i, c, j=j: (0, 0, first + j)) for j in range(pieces)
    ]
    return pl.pallas_call(
        kernel,
        grid_spec=pltpu.PrefetchScalarGridSpec(
            num_scalar_prefetch=1,
            grid=(1,),
            in_specs=specs + specs,
            out_specs=pl.BlockSpec((pieces * width, rhs), lambda i, c: (0, 0)),
        ),
        out_shape=jax.ShapeDtypeStruct((pieces * width, rhs), F32),
        name="unfold",
    )(row, *([mine] * pieces), *([other] * pieces))


def flip(x, axis, size, bits):
    return lax.ppermute(x, axis, [(i, i ^ bits) for i in range(size)])


def pick(index, table, choose):
    distinct = sorted(set(table))
    out = choose(distinct[0])
    for p in distinct[1:]:
        here = False
        for i, q in enumerate(table):
            if q == p:
                here = here | (index == i)
        out = jnp.where(here, choose(p), out)
    return out


def make_shards(nr, nc):
    chips = nr // 2

    def row_sum(x, core):
        half = x.shape[0] // 2
        low, high = x[:half], x[half:]
        mine = jnp.where(core == 0, low, high)
        other = jnp.where(core == 0, high, low).astype(BF)
        mine = mine + flip(other, "row", nr, 1).astype(F32)
        sent = mine.astype(BF)
        for q in range(1, chips):
            mine = mine + flip(sent, "row", nr, 2 * q).astype(F32)
        other = flip(mine, "row", nr, 1)
        return jnp.concatenate(
            [jnp.where(core == 0, mine, other), jnp.where(core == 0, other, mine)], axis=0
        )

    def col_sum_small(x):
        sent = x.astype(BF)
        for q in range(1, nc):
            x = x + flip(sent, "col", nc, q).astype(F32)
        return x

    def col_sum_large(x, col):
        parts = x.reshape(nc, x.shape[0] // nc, x.shape[1])
        total = lax.dynamic_index_in_dim(parts, col, 0, keepdims=False).astype(F32)
        for q in range(1, nc):
            piece = lax.dynamic_index_in_dim(parts, col ^ q, 0, keepdims=False)
            total = total + flip(piece, "col", nc, q).astype(F32)
        total = total.astype(BF)
        got = [total] + [flip(total, "col", nc, q) for q in range(1, nc)]
        tables = [[z ^ p for z in range(nc)] for p in range(nc)]
        return jnp.concatenate([pick(col, t, lambda p: got[p]) for t in tables], axis=0)

    def scatter_chips(keep, got, chip, scale, lanes):
        mine = keep + got.astype(F32)
        total = lax.dynamic_index_in_dim(mine, chip, 0, keepdims=False)
        for q in range(1, chips):
            piece = lax.dynamic_index_in_dim(mine, chip ^ q, 0, keepdims=False).astype(BF)
            total = total + flip(piece, "row", nr, 2 * q).astype(F32)
        factor = jnp.where(jnp.arange(total.shape[1]) < lanes, scale, 1.0).astype(F32)
        return (total * factor[None]).astype(BF)

    def gather_plane(total):
        got = [total] + [flip(total, "row", nr, 2 * q) for q in range(1, chips)]
        mine = jnp.stack(got)
        return mine, flip(mine, "row", nr, 1)

    near = nc // 2

    def position(z, s):
        return nc - 1 - s if z < near else s

    def right_table(t):
        return [position(z, nc - 1 - t + z) if z <= t else None for z in range(nc)]

    def left_table(t):
        return [position(z, t - (nc - 1 - z)) if nc - 1 - z <= t else None for z in range(nc)]

    def filled(table):
        some = [p for p in table if p is not None][0]
        return [some if p is None else p for p in table]

    def line_sends(own, t, got, col):
        sends = []
        for side, table in enumerate((right_table(t), left_table(t))):
            send = pick(col, filled(table), lambda p: own[p])
            if t > 0:
                send = (send.astype(F32) + got[side].astype(F32)).astype(BF)
            sends.append(send)
        return sends

    def line_step(sends, t):
        right = [(z, z + 1) for z in range(nc) if z <= t]
        left = [(z, z - 1) for z in range(nc) if nc - 1 - z <= t]
        if t == 0 and nc > 3:
            got = lax.ppermute(sends[0], "col", right + left)
            return got, got
        return lax.ppermute(sends[0], "col", right), lax.ppermute(sends[1], "col", left)

    def line_last(own, got, col):
        last = pick(col, [position(z, z) for z in range(nc)], lambda p: own[p])
        return last.astype(F32) + got[0].astype(F32) + got[1].astype(F32)

    def steps(residual, diag_inverse, panels, first_block, probe_solved, genotypes, annotation):
        nblk, g, rhs = residual.shape
        row = lax.axis_index("row")
        col = lax.axis_index("col")
        core = row % 2
        chip = row // 2
        snps = annotation.shape[0]
        scale = 1.0 / (snps * nc)
        geno = genotypes.reshape(-1, genotypes.shape[2])
        probe = probe_solved.reshape(-1, rhs)
        block_now = first_block[0]
        row_id = row.astype(jnp.int32)[None]
        col_id = col.astype(jnp.int32)[None]
        barrier = lax.optimization_barrier

        keep0, sent0, keep1, sent1 = project(
            first_block, row_id, probe, diag_inverse, residual, geno, chips
        )
        got0 = flip(sent0, "row", nr, 1)
        got1 = flip(sent1, "row", nr, 1)
        total0 = scatter_chips(keep0, got0, chip, scale, snps)
        total0, got1 = barrier((total0, got1))
        load0 = gather_plane(total0)
        total1 = scatter_chips(keep1, got1, chip, scale, snps)

        ann = annotation.reshape(1, -1)
        per_slice = A // nc

        def partials(load, p, count=2):
            def ids_of(z):
                return [jnp.where(z < near, nc - 1 - s, s) for s in range(p, p + count)]

            return annotate(ids_of, count, row_id, col_id, load[0], load[1], ann, geno, per_slice)

        own0 = partials(load0, 0, nc)
        got0 = line_step(line_sends(own0, 0, None, col), 0)
        total1, own0 = barrier((total1, own0))
        load1 = gather_plane(total1)
        solved_load, own0 = barrier((load0, own0))
        first = unfold(row_id, solved_load[0], solved_load[1], snps, rhs)
        first_bf = first.astype(BF)
        own1 = partials(load1, 0)
        got1 = line_step(line_sends(own1, 0, None, col), 0)
        for t in range(1, nc - 1):
            sends = line_sends(own0, t, got0, col)
            got0 = line_step(sends, t)
            if 2 * t < nc:
                load1, sends = barrier((load1, sends))
                own1 = own1 + partials(load1, 2 * t)
            got1 = line_step(line_sends(own1, t, got1, col), t)
        summed = [line_last(own0, got0, col), line_last(own1, got1, col)]

        next_panel = lax.dynamic_index_in_dim(panels[0], block_now + 1, 0, keepdims=False)
        next_sum = col_sum_small(jnp.dot(next_panel, first_bf, preferred_element_type=F32))
        second_rows = lax.dynamic_index_in_dim(residual, block_now + 1, 0, keepdims=False) - next_sum
        second = row_sum(
            jnp.dot(diag_inverse[1], second_rows.astype(BF), preferred_element_type=F32), core
        )
        second_bf = second.astype(BF)
        late = jnp.arange(2, nblk, dtype=jnp.int32)
        keep_first = (late > block_now).astype(F32)[:, None, None]
        keep_second = (late > block_now + 1).astype(F32)[:, None, None]
        both = keep_first * jnp.einsum(
            "ngc,cr->ngr", panels[0, 2:], first_bf, preferred_element_type=F32
        ) + keep_second * jnp.einsum(
            "ngc,cr->ngr", panels[1, 2:], second_bf, preferred_element_type=F32
        )
        update = col_sum_large(both.astype(BF).reshape(-1, rhs), col).reshape(nblk - 2, g, rhs)
        current = jnp.concatenate([residual[:2], residual[2:] - update.astype(F32)], axis=0)
        spot = jnp.arange(nblk, dtype=jnp.int32)[:, None, None] == block_now + 1
        current = jnp.where(spot, second_rows[None], current)

        half = rhs // 2
        products = jnp.stack(summed, axis=1)
        products = products.reshape(nblk, g, 2, per_slice, half)
        products = jnp.swapaxes(products, 2, 3).reshape(nblk, g, per_slice, rhs).astype(BF)
        return current, jnp.stack([first, second]), products

    return steps


def solution(mesh):
    in_specs = (
        P(None, "row", None),
        P(None, "col", "row"),
        P(None, None, "row", "col"),
        P(),
        P(None, "row", None),
        P(None, "row", "col"),
        P("col"),
    )
    out_specs = (P(None, "row", None), P(None, "col", None), P(None, "row", "col", None))
    shards = make_shards(mesh.shape["row"], mesh.shape["col"])
    return jax.shard_map(shards, mesh=mesh, in_specs=in_specs, out_specs=out_specs, check_vma=False)
```

```python
import jax
import jax.numpy as jnp
from jax import lax
from jax.experimental import pallas as pl
from jax.experimental.pallas import tpu as pltpu
from jax.sharding import PartitionSpec as P


A = 8
BF = jnp.bfloat16
F32 = jnp.float32


def project_kernel(chunks, block_ref, row_ref, probe_hbm, inverse_hbm, residual_hbm, geno_hbm, *rest):
    outs, (geno, probe, inverse, residual, turned, sems) = rest[:4], rest[4:]
    snps = geno.shape[1]
    tile = snps // chunks
    depth = min(3, chunks)

    def copy(i):
        spot = pl.ds(i * tile, tile)
        return pltpu.make_async_copy(geno_hbm.at[:, spot], geno.at[:, spot], sems.at[i])

    inverse_copy = pltpu.make_async_copy(inverse_hbm.at[0], inverse, sems.at[chunks])
    residual_copy = pltpu.make_async_copy(
        residual_hbm.at[block_ref[0]], residual, sems.at[chunks + 1]
    )
    probe_copy = pltpu.make_async_copy(probe_hbm, probe, sems.at[chunks + 2])
    inverse_copy.start()
    residual_copy.start()
    probe_copy.start()
    for i in range(depth):
        copy(i).start()
    core = row_ref[0] % 2
    chips, part = outs[0].shape[0], outs[0].shape[1]
    span = chips * part

    def spread(h, low, high, lanes):
        mine = jnp.where(core == 0, low, high)
        other = jnp.where(core == 0, high, low).astype(BF)
        for q in range(chips):
            rows = slice(q * part, (q + 1) * part)
            outs[2 * h][q, :, lanes] = mine[rows]
            outs[2 * h + 1][q, :, lanes] = other[rows]

    inverse_copy.wait()
    residual_copy.wait()
    solved = jnp.dot(inverse[...], residual[...].astype(BF), preferred_element_type=F32)
    rhs = solved.shape[1]
    for j in range(solved.shape[0] // (2 * span)):
        lanes = slice(snps + j * rhs, snps + (j + 1) * rhs)
        top = 2 * span * j
        spread(0, solved[top : top + span], solved[top + span : top + 2 * span], lanes)
    probe_copy.wait()
    turned[...] = probe[...].T
    for i in range(chunks):
        copy(i).wait()
        if i + depth < chunks:
            copy(i + depth).start()
        lanes = slice(i * tile, (i + 1) * tile)
        acc = jnp.dot(turned[...], geno[:, lanes], preferred_element_type=F32)
        for h in range(2):
            top = 2 * span * h
            spread(h, acc[top : top + span], acc[top + span : top + 2 * span], lanes)


def project(block, row, probe, inverse, residual, geno, chips):
    rows, snps = geno.shape
    rhs = probe.shape[1]
    part = rhs // (4 * chips)
    chunks = 8
    _, m, g = inverse.shape
    extra = m * rhs // (rhs // 2)
    shapes = []
    for wide in (snps + extra, snps):
        shapes += [
            jax.ShapeDtypeStruct((chips, part, wide), F32),
            jax.ShapeDtypeStruct((chips, part, wide), BF),
        ]

    def kernel(*refs):
        project_kernel(chunks, *refs)

    return pl.pallas_call(
        kernel,
        grid_spec=pltpu.PrefetchScalarGridSpec(
            num_scalar_prefetch=2,
            grid=(1,),
            in_specs=[pl.BlockSpec(memory_space=pltpu.HBM)] * 4,
            out_specs=[pl.BlockSpec(s.shape, lambda i, b, c: (0, 0, 0)) for s in shapes],
            scratch_shapes=[
                pltpu.VMEM((rows, snps), BF),
                pltpu.VMEM((rows, rhs), BF),
                pltpu.VMEM((m, g), BF),
                pltpu.VMEM((g, rhs), F32),
                pltpu.VMEM((rhs, rows), BF),
                pltpu.SemaphoreType.DMA((chunks + 3,)),
            ],
        ),
        out_shape=shapes,
        cost_estimate=pl.CostEstimate(
            flops=2 * rows * snps * rhs, bytes_accessed=2 * rows * snps, transcendentals=0
        ),
        name="project",
    )(block, row, probe, inverse, residual, geno)


def annotate_kernel(ids_of, slices, per_slice, row_ref, col_ref, mine_ref, other_ref, ann_ref, geno_ref, *rest):
    outs, (load, weights) = rest[:slices], rest[slices:]
    chips, part, _ = mine_ref.shape
    width = load.shape[0]

    @pl.when(pl.program_id(0) == 0)
    def _():
        core, chip = row_ref[0] % 2, row_ref[0] // 2
        ids = ids_of(col_ref[0])
        for q in range(chips):
            mine = mine_ref[q ^ chip].astype(F32)
            other = other_ref[q ^ chip].astype(F32)
            load[q * part : (q + 1) * part, :] = jnp.where(core == 0, mine, other)
            low = width // 2 + q * part
            load[low : low + part, :] = jnp.where(core == 0, other, mine)
        for s in range(slices):
            for a in range(per_slice):
                here = ann_ref[...] == ids[s] * per_slice + a
                spot = (s * per_slice + a) * width
                weights[spot : spot + width, :] = jnp.where(here, load[...], 0.0).astype(BF)

    wide = per_slice * width
    acc = lax.dot_general(
        geno_ref[...], weights[...], (((1,), (1,)), ((), ())), preferred_element_type=F32
    )
    for s in range(slices):
        outs[s][...] = acc[:, s * wide : (s + 1) * wide].astype(BF)


def annotate(ids_of, slices, row, col, mine, other, ann, geno, per_slice):
    rows, snps = geno.shape
    chips, part, _ = mine.shape
    width = 2 * chips * part
    wide = per_slice * width
    tile = rows // 2

    def kernel(*refs):
        annotate_kernel(ids_of, slices, per_slice, *refs)

    return pl.pallas_call(
        kernel,
        grid_spec=pltpu.PrefetchScalarGridSpec(
            num_scalar_prefetch=2,
            grid=(rows // tile,),
            in_specs=[
                pl.BlockSpec((chips, part, snps), lambda i, c, d: (0, 0, 0)),
                pl.BlockSpec((chips, part, snps), lambda i, c, d: (0, 0, 0)),
                pl.BlockSpec((1, snps), lambda i, c, d: (0, 0)),
                pl.BlockSpec((tile, snps), lambda i, c, d: (i, 0)),
            ],
            out_specs=[pl.BlockSpec((tile, wide), lambda i, c, d: (i, 0))] * slices,
            scratch_shapes=[pltpu.VMEM((width, snps), F32), pltpu.VMEM((slices * wide, snps), BF)],
        ),
        out_shape=[jax.ShapeDtypeStruct((rows, wide), BF)] * slices,
        cost_estimate=pl.CostEstimate(
            flops=2 * rows * snps * slices * wide, bytes_accessed=2 * rows * snps, transcendentals=0
        ),
        name="annotate",
    )(row, col, mine, other, ann, geno)


def unfold(row, mine, other, snps, rhs):
    chips, part, lanes = mine.shape
    width = 2 * chips * part
    pieces = (lanes - snps) // rhs

    def kernel(row_ref, *refs):
        mine_refs, other_refs, out = refs[:pieces], refs[pieces : 2 * pieces], refs[-1]
        core, chip = row_ref[0] % 2, row_ref[0] // 2
        for j in range(pieces):
            for q in range(chips):
                mine_now = mine_refs[j][q ^ chip].astype(F32)
                other_now = other_refs[j][q ^ chip].astype(F32)
                spot = j * width + q * part
                out[spot : spot + part, :] = jnp.where(core == 0, mine_now, other_now)
                spot += width // 2
                out[spot : spot + part, :] = jnp.where(core == 0, other_now, mine_now)

    first = snps // rhs
    specs = [
        pl.BlockSpec((chips, part, rhs), lambda i, c, j=j: (0, 0, first + j)) for j in range(pieces)
    ]
    return pl.pallas_call(
        kernel,
        grid_spec=pltpu.PrefetchScalarGridSpec(
            num_scalar_prefetch=1,
            grid=(1,),
            in_specs=specs + specs,
            out_specs=pl.BlockSpec((pieces * width, rhs), lambda i, c: (0, 0)),
        ),
        out_shape=jax.ShapeDtypeStruct((pieces * width, rhs), F32),
        name="unfold",
    )(row, *([mine] * pieces), *([other] * pieces))


def flip(x, axis, size, bits):
    return lax.ppermute(x, axis, [(i, i ^ bits) for i in range(size)])


def pick(index, table, choose):
    distinct = sorted(set(table))
    out = choose(distinct[0])
    for p in distinct[1:]:
        here = False
        for i, q in enumerate(table):
            if q == p:
                here = here | (index == i)
        out = jnp.where(here, choose(p), out)
    return out


def make_shards(nr, nc):
    chips = nr // 2

    def row_sum(x, core):
        half = x.shape[0] // 2
        low, high = x[:half], x[half:]
        mine = jnp.where(core == 0, low, high)
        other = jnp.where(core == 0, high, low).astype(BF)
        mine = mine + flip(other, "row", nr, 1).astype(F32)
        sent = mine.astype(BF)
        for q in range(1, chips):
            mine = mine + flip(sent, "row", nr, 2 * q).astype(F32)
        other = flip(mine, "row", nr, 1)
        return jnp.concatenate(
            [jnp.where(core == 0, mine, other), jnp.where(core == 0, other, mine)], axis=0
        )

    def col_sum_small(x):
        sent = x.astype(BF)
        for q in range(1, nc):
            x = x + flip(sent, "col", nc, q).astype(F32)
        return x

    def col_sum_large(x, col):
        parts = x.reshape(nc, x.shape[0] // nc, x.shape[1])
        total = lax.dynamic_index_in_dim(parts, col, 0, keepdims=False).astype(F32)
        for q in range(1, nc):
            piece = lax.dynamic_index_in_dim(parts, col ^ q, 0, keepdims=False)
            total = total + flip(piece, "col", nc, q).astype(F32)
        total = total.astype(BF)
        got = [total] + [flip(total, "col", nc, q) for q in range(1, nc)]
        tables = [[z ^ p for z in range(nc)] for p in range(nc)]
        return jnp.concatenate([pick(col, t, lambda p: got[p]) for t in tables], axis=0)

    def scatter_chips(keep, got, chip, scale, lanes):
        mine = keep + got.astype(F32)
        total = lax.dynamic_index_in_dim(mine, chip, 0, keepdims=False)
        for q in range(1, chips):
            piece = lax.dynamic_index_in_dim(mine, chip ^ q, 0, keepdims=False).astype(BF)
            total = total + flip(piece, "row", nr, 2 * q).astype(F32)
        factor = jnp.where(jnp.arange(total.shape[1]) < lanes, scale, 1.0).astype(F32)
        return (total * factor[None]).astype(BF)

    def gather_plane(total):
        got = [total] + [flip(total, "row", nr, 2 * q) for q in range(1, chips)]
        mine = jnp.stack(got)
        return mine, flip(mine, "row", nr, 1)

    near = nc // 2

    def slice_order(z):
        if nc == 4:
            return [[3, 2, 1, 0], [0, 3, 2, 1], [3, 0, 1, 2], [0, 1, 2, 3]][z]
        return [nc - 1 - p if z < near else p for p in range(nc)]

    orders = [slice_order(z) for z in range(nc)]

    def right_table(t):
        return [orders[z].index(nc - 1 - t + z) if z <= t else None for z in range(nc)]

    def left_table(t):
        return [orders[z].index(t - (nc - 1 - z)) if nc - 1 - z <= t else None for z in range(nc)]

    def filled(table):
        some = [p for p in table if p is not None][0]
        return [some if p is None else p for p in table]

    def line_sends(own, t, got, col):
        right, left = right_table(t), left_table(t)
        if t < near and (t == 0 or got[0] is got[1]):
            tables = [[p if q is None else q for p, q in zip(right, left)]]
        else:
            tables = [right, left]
        sends = []
        for side, table in enumerate(tables):
            send = pick(col, filled(table), lambda p: own[p])
            if t > 0:
                send = (send.astype(F32) + got[side].astype(F32)).astype(BF)
            sends.append(send)
        return sends if len(sends) == 2 else sends * 2

    def line_step(sends, t):
        right = [(z, z + 1) for z in range(nc) if z <= t]
        left = [(z, z - 1) for z in range(nc) if nc - 1 - z <= t]
        if t == 0 and nc > 3:
            got = lax.ppermute(sends[0], "col", right + left)
            return got, got
        return lax.ppermute(sends[0], "col", right), lax.ppermute(sends[1], "col", left)

    def line_last(own, got, col):
        last = pick(col, [orders[z].index(z) for z in range(nc)], lambda p: own[p])
        return last.astype(F32) + got[0].astype(F32) + got[1].astype(F32)

    def steps(residual, diag_inverse, panels, first_block, probe_solved, genotypes, annotation):
        nblk, g, rhs = residual.shape
        row = lax.axis_index("row")
        col = lax.axis_index("col")
        core = row % 2
        chip = row // 2
        snps = annotation.shape[0]
        scale = 1.0 / (snps * nc)
        geno = genotypes.reshape(-1, genotypes.shape[2])
        probe = probe_solved.reshape(-1, rhs)
        block_now = first_block[0]
        row_id = row.astype(jnp.int32)[None]
        col_id = col.astype(jnp.int32)[None]
        barrier = lax.optimization_barrier

        keep0, sent0, keep1, sent1 = project(
            first_block, row_id, probe, diag_inverse, residual, geno, chips
        )
        got0 = flip(sent0, "row", nr, 1)
        got1 = flip(sent1, "row", nr, 1)
        total0 = scatter_chips(keep0, got0, chip, scale, snps)
        total0, got1 = barrier((total0, got1))
        load0 = gather_plane(total0)
        total1 = scatter_chips(keep1, got1, chip, scale, snps)

        ann = annotation.reshape(1, -1)
        per_slice = A // nc

        def partials(load, p, count=2):
            def ids_of(z):
                return [pick(z, [o[s] for o in orders], lambda v: jnp.int32(v)) for s in range(p, p + count)]

            return annotate(ids_of, count, row_id, col_id, load[0], load[1], ann, geno, per_slice)

        own0 = partials(load0, 0, nc)
        got0 = line_step(line_sends(own0, 0, None, col), 0)
        total1, own0 = barrier((total1, own0))
        load1 = gather_plane(total1)
        solved_load, own0 = barrier((load0, own0))
        first = unfold(row_id, solved_load[0], solved_load[1], snps, rhs)
        first_bf = first.astype(BF)
        own1 = partials(load1, 0)
        got1 = line_step(line_sends(own1, 0, None, col), 0)
        for t in range(1, nc - 1):
            sends = line_sends(own0, t, got0, col)
            got0 = line_step(sends, t)
            if 2 * t < nc:
                load1, sends = barrier((load1, sends))
                own1 = own1 + partials(load1, 2 * t)
            got1 = line_step(line_sends(own1, t, got1, col), t)
        summed = [line_last(own0, got0, col), line_last(own1, got1, col)]

        next_panel = lax.dynamic_index_in_dim(panels[0], block_now + 1, 0, keepdims=False)
        next_sum = col_sum_small(jnp.dot(next_panel, first_bf, preferred_element_type=F32))
        second_rows = lax.dynamic_index_in_dim(residual, block_now + 1, 0, keepdims=False) - next_sum
        second = row_sum(
            jnp.dot(diag_inverse[1], second_rows.astype(BF), preferred_element_type=F32), core
        )
        second_bf = second.astype(BF)
        late = jnp.arange(2, nblk, dtype=jnp.int32)
        keep_first = (late > block_now).astype(F32)[:, None, None]
        keep_second = (late > block_now + 1).astype(F32)[:, None, None]
        both = keep_first * jnp.einsum(
            "ngc,cr->ngr", panels[0, 2:], first_bf, preferred_element_type=F32
        ) + keep_second * jnp.einsum(
            "ngc,cr->ngr", panels[1, 2:], second_bf, preferred_element_type=F32
        )
        update = col_sum_large(both.astype(BF).reshape(-1, rhs), col).reshape(nblk - 2, g, rhs)
        current = jnp.concatenate([residual[:2], residual[2:] - update.astype(F32)], axis=0)
        spot = jnp.arange(nblk, dtype=jnp.int32)[:, None, None] == block_now + 1
        current = jnp.where(spot, second_rows[None], current)

        half = rhs // 2
        products = jnp.stack(summed, axis=1)
        products = products.reshape(nblk, g, 2, per_slice, half)
        products = jnp.swapaxes(products, 2, 3).reshape(nblk, g, per_slice, rhs).astype(BF)
        return current, jnp.stack([first, second]), products

    return steps


def solution(mesh):
    in_specs = (
        P(None, "row", None),
        P(None, "col", "row"),
        P(None, None, "row", "col"),
        P(),
        P(None, "row", None),
        P(None, "row", "col"),
        P("col"),
    )
    out_specs = (P(None, "row", None), P(None, "col", None), P(None, "row", "col", None))
    shards = make_shards(mesh.shape["row"], mesh.shape["col"])
    return jax.shard_map(shards, mesh=mesh, in_specs=in_specs, out_specs=out_specs, check_vma=False)
```

```python
import jax
import jax.numpy as jnp
from jax import lax
from jax.experimental import pallas as pl
from jax.experimental.pallas import tpu as pltpu
from jax.sharding import PartitionSpec as P


A = 8
BF = jnp.bfloat16
F32 = jnp.float32


def project_kernel(chunks, block_ref, row_ref, probe_hbm, inverse_hbm, residual_hbm, geno_hbm, *rest):
    outs, (geno, probe, inverse, residual, turned, sems) = rest[:4], rest[4:]
    snps = geno.shape[1]
    tile = snps // chunks
    depth = min(3, chunks)

    def copy(i):
        spot = pl.ds(i * tile, tile)
        return pltpu.make_async_copy(geno_hbm.at[:, spot], geno.at[:, spot], sems.at[i])

    inverse_copy = pltpu.make_async_copy(inverse_hbm.at[0], inverse, sems.at[chunks])
    residual_copy = pltpu.make_async_copy(
        residual_hbm.at[block_ref[0]], residual, sems.at[chunks + 1]
    )
    probe_copy = pltpu.make_async_copy(probe_hbm, probe, sems.at[chunks + 2])
    inverse_copy.start()
    residual_copy.start()
    probe_copy.start()
    for i in range(depth):
        copy(i).start()
    core = row_ref[0] % 2
    chips, part = outs[0].shape[0], outs[0].shape[1]
    span = chips * part

    def spread(h, low, high, lanes):
        mine = jnp.where(core == 0, low, high)
        other = jnp.where(core == 0, high, low).astype(BF)
        for q in range(chips):
            rows = slice(q * part, (q + 1) * part)
            outs[2 * h][q, :, lanes] = mine[rows]
            outs[2 * h + 1][q, :, lanes] = other[rows]

    inverse_copy.wait()
    residual_copy.wait()
    solved = jnp.dot(inverse[...], residual[...].astype(BF), preferred_element_type=F32)
    rhs = solved.shape[1]
    for j in range(solved.shape[0] // (2 * span)):
        lanes = slice(snps + j * rhs, snps + (j + 1) * rhs)
        top = 2 * span * j
        spread(0, solved[top : top + span], solved[top + span : top + 2 * span], lanes)
    probe_copy.wait()
    turned[...] = probe[...].T
    for i in range(chunks):
        copy(i).wait()
        if i + depth < chunks:
            copy(i + depth).start()
        lanes = slice(i * tile, (i + 1) * tile)
        acc = jnp.dot(turned[...], geno[:, lanes], preferred_element_type=F32)
        for h in range(2):
            top = 2 * span * h
            spread(h, acc[top : top + span], acc[top + span : top + 2 * span], lanes)


def project(block, row, probe, inverse, residual, geno, chips):
    rows, snps = geno.shape
    rhs = probe.shape[1]
    part = rhs // (4 * chips)
    chunks = 8
    _, m, g = inverse.shape
    extra = m * rhs // (rhs // 2)
    shapes = []
    for wide in (snps + extra, snps):
        shapes += [
            jax.ShapeDtypeStruct((chips, part, wide), F32),
            jax.ShapeDtypeStruct((chips, part, wide), BF),
        ]

    def kernel(*refs):
        project_kernel(chunks, *refs)

    return pl.pallas_call(
        kernel,
        grid_spec=pltpu.PrefetchScalarGridSpec(
            num_scalar_prefetch=2,
            grid=(1,),
            in_specs=[pl.BlockSpec(memory_space=pltpu.HBM)] * 4,
            out_specs=[pl.BlockSpec(s.shape, lambda i, b, c: (0, 0, 0)) for s in shapes],
            scratch_shapes=[
                pltpu.VMEM((rows, snps), BF),
                pltpu.VMEM((rows, rhs), BF),
                pltpu.VMEM((m, g), BF),
                pltpu.VMEM((g, rhs), F32),
                pltpu.VMEM((rhs, rows), BF),
                pltpu.SemaphoreType.DMA((chunks + 3,)),
            ],
        ),
        out_shape=shapes,
        cost_estimate=pl.CostEstimate(
            flops=2 * rows * snps * rhs, bytes_accessed=2 * rows * snps, transcendentals=0
        ),
        name="project",
    )(block, row, probe, inverse, residual, geno)


def annotate_kernel(ids_of, slices, per_slice, row_ref, col_ref, mine_ref, other_ref, ann_ref, geno_ref, *rest):
    outs, (load, weights) = rest[:slices], rest[slices:]
    chips, part, _ = mine_ref.shape
    width = load.shape[0]

    @pl.when(pl.program_id(0) == 0)
    def _():
        core, chip = row_ref[0] % 2, row_ref[0] // 2
        ids = ids_of(col_ref[0])
        for q in range(chips):
            mine = mine_ref[q ^ chip].astype(F32)
            other = other_ref[q ^ chip].astype(F32)
            load[q * part : (q + 1) * part, :] = jnp.where(core == 0, mine, other)
            low = width // 2 + q * part
            load[low : low + part, :] = jnp.where(core == 0, other, mine)
        for s in range(slices):
            for a in range(per_slice):
                here = ann_ref[...] == ids[s] * per_slice + a
                spot = (s * per_slice + a) * width
                weights[spot : spot + width, :] = jnp.where(here, load[...], 0.0).astype(BF)

    wide = per_slice * width
    acc = lax.dot_general(
        geno_ref[...], weights[...], (((1,), (1,)), ((), ())), preferred_element_type=F32
    )
    for s in range(slices):
        outs[s][...] = acc[:, s * wide : (s + 1) * wide].astype(BF)


def annotate(ids_of, slices, row, col, mine, other, ann, geno, per_slice):
    rows, snps = geno.shape
    chips, part, _ = mine.shape
    width = 2 * chips * part
    wide = per_slice * width
    tile = rows // 4

    def kernel(*refs):
        annotate_kernel(ids_of, slices, per_slice, *refs)

    return pl.pallas_call(
        kernel,
        grid_spec=pltpu.PrefetchScalarGridSpec(
            num_scalar_prefetch=2,
            grid=(rows // tile,),
            in_specs=[
                pl.BlockSpec((chips, part, snps), lambda i, c, d: (0, 0, 0)),
                pl.BlockSpec((chips, part, snps), lambda i, c, d: (0, 0, 0)),
                pl.BlockSpec((1, snps), lambda i, c, d: (0, 0)),
                pl.BlockSpec((tile, snps), lambda i, c, d: (i, 0)),
            ],
            out_specs=[pl.BlockSpec((tile, wide), lambda i, c, d: (i, 0))] * slices,
            scratch_shapes=[pltpu.VMEM((width, snps), F32), pltpu.VMEM((slices * wide, snps), BF)],
        ),
        out_shape=[jax.ShapeDtypeStruct((rows, wide), BF)] * slices,
        cost_estimate=pl.CostEstimate(
            flops=2 * rows * snps * slices * wide, bytes_accessed=2 * rows * snps, transcendentals=0
        ),
        name="annotate",
    )(row, col, mine, other, ann, geno)


def unfold(row, mine, other, snps, rhs):
    chips, part, lanes = mine.shape
    width = 2 * chips * part
    pieces = (lanes - snps) // rhs

    def kernel(row_ref, *refs):
        mine_refs, other_refs, out = refs[:pieces], refs[pieces : 2 * pieces], refs[-1]
        core, chip = row_ref[0] % 2, row_ref[0] // 2
        for j in range(pieces):
            for q in range(chips):
                mine_now = mine_refs[j][q ^ chip].astype(F32)
                other_now = other_refs[j][q ^ chip].astype(F32)
                spot = j * width + q * part
                out[spot : spot + part, :] = jnp.where(core == 0, mine_now, other_now)
                spot += width // 2
                out[spot : spot + part, :] = jnp.where(core == 0, other_now, mine_now)

    first = snps // rhs
    specs = [
        pl.BlockSpec((chips, part, rhs), lambda i, c, j=j: (0, 0, first + j)) for j in range(pieces)
    ]
    return pl.pallas_call(
        kernel,
        grid_spec=pltpu.PrefetchScalarGridSpec(
            num_scalar_prefetch=1,
            grid=(1,),
            in_specs=specs + specs,
            out_specs=pl.BlockSpec((pieces * width, rhs), lambda i, c: (0, 0)),
        ),
        out_shape=jax.ShapeDtypeStruct((pieces * width, rhs), F32),
        name="unfold",
    )(row, *([mine] * pieces), *([other] * pieces))


def flip(x, axis, size, bits):
    return lax.ppermute(x, axis, [(i, i ^ bits) for i in range(size)])


def pick(index, table, choose):
    distinct = sorted(set(table))
    out = choose(distinct[0])
    for p in distinct[1:]:
        here = False
        for i, q in enumerate(table):
            if q == p:
                here = here | (index == i)
        out = jnp.where(here, choose(p), out)
    return out


def make_shards(nr, nc):
    chips = nr // 2

    def row_sum(x, core):
        half = x.shape[0] // 2
        low, high = x[:half], x[half:]
        mine = jnp.where(core == 0, low, high)
        other = jnp.where(core == 0, high, low).astype(BF)
        mine = mine + flip(other, "row", nr, 1).astype(F32)
        sent = mine.astype(BF)
        for q in range(1, chips):
            mine = mine + flip(sent, "row", nr, 2 * q).astype(F32)
        other = flip(mine, "row", nr, 1)
        return jnp.concatenate(
            [jnp.where(core == 0, mine, other), jnp.where(core == 0, other, mine)], axis=0
        )

    def col_sum_small(x):
        sent = x.astype(BF)
        for q in range(1, nc):
            x = x + flip(sent, "col", nc, q).astype(F32)
        return x

    def col_sum_large(x, col):
        parts = x.reshape(nc, x.shape[0] // nc, x.shape[1])
        total = lax.dynamic_index_in_dim(parts, col, 0, keepdims=False).astype(F32)
        for q in range(1, nc):
            piece = lax.dynamic_index_in_dim(parts, col ^ q, 0, keepdims=False)
            total = total + flip(piece, "col", nc, q).astype(F32)
        total = total.astype(BF)
        got = [total] + [flip(total, "col", nc, q) for q in range(1, nc)]
        tables = [[z ^ p for z in range(nc)] for p in range(nc)]
        return jnp.concatenate([pick(col, t, lambda p: got[p]) for t in tables], axis=0)

    def scatter_chips(keep, got, chip, scale, lanes):
        mine = keep + got.astype(F32)
        total = lax.dynamic_index_in_dim(mine, chip, 0, keepdims=False)
        for q in range(1, chips):
            piece = lax.dynamic_index_in_dim(mine, chip ^ q, 0, keepdims=False).astype(BF)
            total = total + flip(piece, "row", nr, 2 * q).astype(F32)
        factor = jnp.where(jnp.arange(total.shape[1]) < lanes, scale, 1.0).astype(F32)
        return (total * factor[None]).astype(BF)

    def gather_plane(total):
        got = [total] + [flip(total, "row", nr, 2 * q) for q in range(1, chips)]
        mine = jnp.stack(got)
        return mine, flip(mine, "row", nr, 1)

    near = nc // 2

    def slice_order(z):
        if nc == 4:
            return [[3, 2, 1, 0], [0, 3, 2, 1], [3, 0, 1, 2], [0, 1, 2, 3]][z]
        return [nc - 1 - p if z < near else p for p in range(nc)]

    orders = [slice_order(z) for z in range(nc)]

    def right_table(t):
        return [orders[z].index(nc - 1 - t + z) if z <= t else None for z in range(nc)]

    def left_table(t):
        return [orders[z].index(t - (nc - 1 - z)) if nc - 1 - z <= t else None for z in range(nc)]

    def filled(table):
        some = [p for p in table if p is not None][0]
        return [some if p is None else p for p in table]

    def line_sends(own, t, got, col):
        right, left = right_table(t), left_table(t)
        if t < near and (t == 0 or got[0] is got[1]):
            tables = [[p if q is None else q for p, q in zip(right, left)]]
        else:
            tables = [right, left]
        sends = []
        for side, table in enumerate(tables):
            send = pick(col, filled(table), lambda p: own[p])
            if t > 0:
                send = (send.astype(F32) + got[side].astype(F32)).astype(BF)
            sends.append(send)
        return sends if len(sends) == 2 else sends * 2

    def line_step(sends, t):
        right = [(z, z + 1) for z in range(nc) if z <= t]
        left = [(z, z - 1) for z in range(nc) if nc - 1 - z <= t]
        if t == 0 and nc > 3:
            got = lax.ppermute(sends[0], "col", right + left)
            return got, got
        return lax.ppermute(sends[0], "col", right), lax.ppermute(sends[1], "col", left)

    def line_last(own, got, col):
        last = pick(col, [orders[z].index(z) for z in range(nc)], lambda p: own[p])
        return last.astype(F32) + got[0].astype(F32) + got[1].astype(F32)

    def steps(residual, diag_inverse, panels, first_block, probe_solved, genotypes, annotation):
        nblk, g, rhs = residual.shape
        row = lax.axis_index("row")
        col = lax.axis_index("col")
        core = row % 2
        chip = row // 2
        snps = annotation.shape[0]
        scale = 1.0 / (snps * nc)
        geno = genotypes.reshape(-1, genotypes.shape[2])
        probe = probe_solved.reshape(-1, rhs)
        block_now = first_block[0]
        row_id = row.astype(jnp.int32)[None]
        col_id = col.astype(jnp.int32)[None]
        barrier = lax.optimization_barrier

        keep0, sent0, keep1, sent1 = project(
            first_block, row_id, probe, diag_inverse, residual, geno, chips
        )
        got0 = flip(sent0, "row", nr, 1)
        got1 = flip(sent1, "row", nr, 1)
        total0 = scatter_chips(keep0, got0, chip, scale, snps)
        total0, got1 = barrier((total0, got1))
        load0 = gather_plane(total0)
        total1 = scatter_chips(keep1, got1, chip, scale, snps)

        ann = annotation.reshape(1, -1)
        per_slice = A // nc

        def partials(load, p, count=2):
            def ids_of(z):
                return [pick(z, [o[s] for o in orders], lambda v: jnp.int32(v)) for s in range(p, p + count)]

            return annotate(ids_of, count, row_id, col_id, load[0], load[1], ann, geno, per_slice)

        own0 = partials(load0, 0, nc)
        got0 = line_step(line_sends(own0, 0, None, col), 0)
        total1, own0 = barrier((total1, own0))
        load1 = gather_plane(total1)
        solved_load, own0 = barrier((load0, own0))
        first = unfold(row_id, solved_load[0], solved_load[1], snps, rhs)
        first_bf = first.astype(BF)
        own1 = partials(load1, 0, nc)
        got1 = line_step(line_sends(own1, 0, None, col), 0)
        for t in range(1, nc - 1):
            sends = line_sends(own0, t, got0, col)
            got0 = line_step(sends, t)
            got1 = line_step(line_sends(own1, t, got1, col), t)
        summed = [line_last(own0, got0, col), line_last(own1, got1, col)]

        next_panel = lax.dynamic_index_in_dim(panels[0], block_now + 1, 0, keepdims=False)
        next_sum = col_sum_small(jnp.dot(next_panel, first_bf, preferred_element_type=F32))
        second_rows = lax.dynamic_index_in_dim(residual, block_now + 1, 0, keepdims=False) - next_sum
        second = row_sum(
            jnp.dot(diag_inverse[1], second_rows.astype(BF), preferred_element_type=F32), core
        )
        second_bf = second.astype(BF)
        late = jnp.arange(2, nblk, dtype=jnp.int32)
        keep_first = (late > block_now).astype(F32)[:, None, None]
        keep_second = (late > block_now + 1).astype(F32)[:, None, None]
        both = keep_first * jnp.einsum(
            "ngc,cr->ngr", panels[0, 2:], first_bf, preferred_element_type=F32
        ) + keep_second * jnp.einsum(
            "ngc,cr->ngr", panels[1, 2:], second_bf, preferred_element_type=F32
        )
        update = col_sum_large(both.astype(BF).reshape(-1, rhs), col).reshape(nblk - 2, g, rhs)
        current = jnp.concatenate([residual[:2], residual[2:] - update.astype(F32)], axis=0)
        spot = jnp.arange(nblk, dtype=jnp.int32)[:, None, None] == block_now + 1
        current = jnp.where(spot, second_rows[None], current)

        half = rhs // 2
        products = jnp.stack(summed, axis=1)
        products = products.reshape(nblk, g, 2, per_slice, half)
        products = jnp.swapaxes(products, 2, 3).reshape(nblk, g, per_slice, rhs).astype(BF)
        return current, jnp.stack([first, second]), products

    return steps


def solution(mesh):
    in_specs = (
        P(None, "row", None),
        P(None, "col", "row"),
        P(None, None, "row", "col"),
        P(),
        P(None, "row", None),
        P(None, "row", "col"),
        P("col"),
    )
    out_specs = (P(None, "row", None), P(None, "col", None), P(None, "row", "col", None))
    shards = make_shards(mesh.shape["row"], mesh.shape["col"])
    return jax.shard_map(shards, mesh=mesh, in_specs=in_specs, out_specs=out_specs, check_vma=False)
```
